32 devices in a mesh: wa: 8 (over z, x), sa: 4 (over y, core).
Axes of the slice: x: 2, y: 2, z: 4, core: 2. Of those that a mesh axis runs over, the one named last changes fastest.
Arguments:
- unit_entry_lines: bfloat16 [4096, 1024], P(('wa', 'sa')), may hold values from -6 to 6
- opening_stratum_contents: bfloat16 [4096, 1024], P(('wa', 'sa')), may hold values from -6 to 6
- packed_sequence_ids: int32 [4096], P(('wa', 'sa')), may hold values from 0 to 15, never falling along the last dimension, each value on 1 to 512 neighbouring positions
- unit_exit_slope: bfloat16 [4096, 1024], P(('wa', 'sa')), may hold values from -6 to 6
- earlier_norming_amplitude_arg: bfloat16 [1024], P('wa'), may hold values from 0.5 to 1.5
- earlier_norming_offset_arg: bfloat16 [1024], P('wa'), may hold values from -1.5 to 1.5
- token_lag_blends: bfloat16 [6144], P('wa'), may hold values from 0 to 1
- acceptor_mapping: bfloat16 [1048576], P('wa'), may hold values from -0.1875 to 0.1875
- lookup_mapping: bfloat16 [1048576], P('wa'), may hold values from -0.1875 to 0.1875
- content_mapping: bfloat16 [1048576], P('wa'), may hold values from -0.1875 to 0.1875
- exit_mapping: bfloat16 [1048576], P('wa'), may hold values from -0.375 to 0.375
- fading_feature_odds: bfloat16 [1024], P('wa'), may hold values from -12 to 2
- fading_leftside_array: bfloat16 [65536], P('wa'), may hold values from -0.1875 to 0.1875
- fading_rightside_array: bfloat16 [65536], P('wa'), may hold values from -0.375 to 0.375
- learning_speed_odds: bfloat16 [1024], P('wa'), may hold values from -4 to 4
- speed_leftside_array: bfloat16 [65536], P('wa'), may hold values from -0.1875 to 0.1875
- speed_rightside_array: bfloat16 [65536], P('wa'), may hold values from -0.75 to 0.75
- content_skip_odds: bfloat16 [1024], P('wa'), may hold values from -4 to 4
- content_skip_leftside: bfloat16 [32768], P('wa'), may hold values from -0.1875 to 0.1875
- content_skip_rightside: bfloat16 [32768], P('wa'), may hold values from -1 to 1
- valve_leftside_array: bfloat16 [163840], P('wa'), may hold values from -0.1875 to 0.1875
- valve_rightside_array: bfloat16 [163840], P('wa'), may hold values from -0.5 to 0.5
- erasure_lookup_stretch: bfloat16 [1024], P('wa'), may hold values from 0.29882812 to 1.5
- stored_lookup_speed: bfloat16 [1024], P('wa'), may hold values from 0.19921875 to 1.796875
- present_token_boost: bfloat16 [1024], P('wa'), may hold values from -3 to 3
- cluster_norming_amplitude_array: bfloat16 [1024], P('wa'), may hold values from 0.5 to 1.5
- cluster_norming_offset_array: bfloat16 [1024], P('wa'), may hold values from -1.5 to 1.5
- later_norming_amplitude_arg: bfloat16 [1024], P('wa'), may hold values from 0.5 to 1.5
- later_norming_offset_arg: bfloat16 [1024], P('wa'), may hold values from -1.5 to 1.5
- feature_lag_blend: bfloat16 [1024], P('wa'), may hold values from 0 to 1
- perceptron_lookup_array: bfloat16 [4194304], P('wa'), may hold values from -0.1875 to 0.1875
- perceptron_content_array: bfloat16 [4194304], P('wa'), may hold values from -0.09375 to 0.09375
Outputs:
- block_out: bfloat16 [4096, 1024], P(('wa', 'sa'))
- grad_block_in: float32 [4096, 1024], P(('wa', 'sa'))
- grad_value_first: float32 [4096, 1024], P(('wa', 'sa'))
- grad_ln1_gain: float32 [1024], P('wa')
- grad_ln1_bias: float32 [1024], P('wa')
- grad_mix_time: float32 [6144], P('wa')
- grad_w_receptance: float32 [1048576], P('wa')
- grad_w_key: float32 [1048576], P('wa')
- grad_w_value: float32 [1048576], P('wa')
- grad_w_output: float32 [1048576], P('wa')
- grad_decay_base: float32 [1024], P('wa')
- grad_decay_down: float32 [65536], P('wa')
- decay_second_factor_gradient: float32 [65536], P('wa')
- grad_rate_base: float32 [1024], P('wa')
- grad_rate_down: float32 [65536], P('wa')
- rate_second_factor_gradient: float32 [65536], P('wa')
- value_residual_logits_gradient: float32 [1024], P('wa')
- value_residual_first_gradient: float32 [32768], P('wa')
- value_residual_second_gradient: float32 [32768], P('wa')
- grad_gate_down: float32 [163840], P('wa')
- grad_gate_up: float32 [163840], P('wa')
- grad_key_norm: float32 [1024], P('wa')
- grad_key_rate: float32 [1024], P('wa')
- present_token_boost_slope: float32 [1024], P('wa')
- grad_lnx_gain: float32 [1024], P('wa')
- grad_lnx_bias: float32 [1024], P('wa')
- grad_ln2_gain: float32 [1024], P('wa')
- grad_ln2_bias: float32 [1024], P('wa')
- grad_mix_channel: float32 [1024], P('wa')
- grad_ffn_key: float32 [4194304], P('wa')
- grad_ffn_value: float32 [4194304], P('wa')
The draws below stay inside these ranges and needn't reach their ends.
Inputs may be any that keep to these rules, and one draw needn't show every extreme that they name: `packed_sequence_ids`: segment numbers never fall along the tokens; a segment holds 1 to 512 tokens and may run over a sequence's start.
All inputs are finite; a program needn't handle non-finite values.
Results may differ from the reference program's by a relative error of at most 0.015.
The reference program's roundings to bfloat16 on the way count: a program that leaves them out, or rounds other values in their place, can miss the bound.
Values may be sent and summed in bfloat16 or wider, within the bound.
A program may use at most 256 MiB of HBM per device.

```python
import math
import jax
import jax.numpy as jnp
import numpy as np
from jax import lax

NETWORK_WIDTH = 1024
HEAD_SIZE = 64
FEEDFORWARD_UNITS = 4096
DECAY_INNER = 64
RATE_INNER = 64
VALUE_RES_INNER = 32
GATE_INNER = 160
TOK_DEV = 128
SEQ = 512
TOKENS = 4096


DECAY_FACTOR = 0.606531


def draw_fading_feature_odds(key, part):
    bottom = math.log(0.3 / SEQ)
    ceiling = math.log(0.5)
    variance_width = jax.random.uniform(key, (NETWORK_WIDTH,), jnp.float32, bottom, ceiling)
    fraction = jnp.exp(variance_width) / DECAY_FACTOR
    return jnp.log(fraction / (1.0 - fraction)).astype(jnp.bfloat16)


def levels(own_key, extent, shards, smallest, high):
    def one(axis_at, parts):
        heights = jax.random.uniform(jax.random.fold_in(jax.random.fold_in(own_key, 6), axis_at), (parts,), jnp.float32, smallest / len(shards), high / len(shards))
        return jnp.repeat(jnp.exp(heights), extent[axis_at] // parts).reshape((-1,) + (1,) * (len(extent) - axis_at - 1))

    level = one(*shards[0])
    for cut in shards[1:]:
        level = level * one(*cut)
    return level


def profile(number_of, total, most, lean):
    loads = [(1 << 20) // math.isqrt(rank ** lean) + 1 for rank in range(2, number_of + 1)]
    surplus, given = total - most - (number_of - 1), [1] * (number_of - 1)
    while surplus > 0:
        movable = [i for i in range(number_of - 1) if given[i] < most]
        pool, budget = sum([loads[i] for i in movable]), surplus
        for i in movable:
            more = min(most - given[i], max(1, budget * loads[i] // pool), surplus)
            given[i] = given[i] + more
            surplus = surplus - more
    return np.array([most] + given)


def uneven(stream_key, count, total, limit, lean):
    if count == 2:
        one = jax.random.randint(stream_key, (), max(1, total - limit), min(limit, total - 1) + 1)
        return jnp.stack([one, total - one])
    sizes = jnp.asarray(profile(count, total, limit, lean), jnp.int32)
    twos = (count - 1) // 2
    giver, receiver = sizes[1:1 + 2 * twos:2], sizes[2:2 + 2 * twos:2]
    room = jnp.minimum(giver - 1, limit - receiver)
    moved = jax.random.randint(jax.random.fold_in(stream_key, 1), (twos,), 0, 1 << 20) % (room + 1)
    sizes = sizes.at[1:1 + 2 * twos:2].set(giver - moved).at[2:2 + 2 * twos:2].set(receiver + moved)
    return sizes[jax.random.permutation(jax.random.fold_in(stream_key, 2), count)]


def bell_draw(own_key, shape, width, bound, cuts=(), kind=jnp.bfloat16):
    values = width * jax.random.normal(own_key, shape, jnp.float32)
    if cuts:
        values = values * levels(own_key, shape, cuts, -0.22, 0.18)
    return jnp.clip(values, -bound, bound).astype(kind)


def setup_inputs(seed: int = 0) -> dict:
    key_of = jax.random.split(jax.random.key(seed), 33)
    return {
        "unit_entry_lines": bell_draw(key_of[0], (TOKENS, NETWORK_WIDTH), 1.0, 6.0, ((0, 32),)),
        "opening_stratum_contents": bell_draw(key_of[1], (TOKENS, NETWORK_WIDTH), 1.0, 6.0, ((0, 32),)),
        "packed_sequence_ids": jnp.searchsorted(jnp.cumsum(uneven(key_of[2], TOKENS // (2 * TOK_DEV), TOKENS, SEQ, 1)), jnp.arange(TOKENS), side="right").astype(jnp.int32),
        "unit_exit_slope": bell_draw(key_of[3], (TOKENS, NETWORK_WIDTH), 1.0, 6.0, ((0, 32),)),
        "earlier_norming_amplitude_arg": jnp.clip(1.0 + 0.1 * jax.random.normal(key_of[4], (NETWORK_WIDTH,), jnp.float32), 0.5, 1.5).astype(jnp.bfloat16),
        "earlier_norming_offset_arg": bell_draw(key_of[5], (NETWORK_WIDTH,), 0.3, 1.5, ((0, 8),)),
        "token_lag_blends": jnp.clip(1.0 * jax.random.uniform(key_of[6], (6 * NETWORK_WIDTH,), jnp.float32) ** levels(key_of[6], (6 * NETWORK_WIDTH,), ((0, 8),), -0.2, 0.2), 0.0, 1.0).astype(jnp.bfloat16),
        "acceptor_mapping": bell_draw(key_of[7], (NETWORK_WIDTH * NETWORK_WIDTH,), NETWORK_WIDTH ** -0.5, 0.1875, ((0, 8),)),
        "lookup_mapping": bell_draw(key_of[8], (NETWORK_WIDTH * NETWORK_WIDTH,), NETWORK_WIDTH ** -0.5, 0.1875, ((0, 8),)),
        "content_mapping": bell_draw(key_of[9], (NETWORK_WIDTH * NETWORK_WIDTH,), NETWORK_WIDTH ** -0.5, 0.1875, ((0, 8),)),
        "exit_mapping": bell_draw(key_of[10], (NETWORK_WIDTH * NETWORK_WIDTH,), (NETWORK_WIDTH // 4) ** -0.5, 0.375, ((0, 8),)),
        "fading_feature_odds": draw_fading_feature_odds(jax.random.fold_in(key_of[32], 71), 0),
        "fading_leftside_array": bell_draw(key_of[12], (NETWORK_WIDTH * DECAY_INNER,), NETWORK_WIDTH ** -0.5, 0.1875, ((0, 8),)),
        "fading_rightside_array": bell_draw(key_of[13], (DECAY_INNER * NETWORK_WIDTH,), (4 * DECAY_INNER) ** -0.5, 0.375, ((0, 8),)),
        "learning_speed_odds": bell_draw(key_of[14], (NETWORK_WIDTH,), 1.0, 4.0, ((0, 8),)),
        "speed_leftside_array": bell_draw(key_of[15], (NETWORK_WIDTH * RATE_INNER,), NETWORK_WIDTH ** -0.5, 0.1875, ((0, 8),)),
        "speed_rightside_array": bell_draw(key_of[16], (RATE_INNER * NETWORK_WIDTH,), RATE_INNER ** -0.5, 0.75, ((0, 8),)),
        "content_skip_odds": bell_draw(key_of[17], (NETWORK_WIDTH,), 1.0, 4.0, ((0, 8),)),
        "content_skip_leftside": bell_draw(key_of[18], (NETWORK_WIDTH * VALUE_RES_INNER,), NETWORK_WIDTH ** -0.5, 0.1875, ((0, 8),)),
        "content_skip_rightside": bell_draw(key_of[19], (VALUE_RES_INNER * NETWORK_WIDTH,), VALUE_RES_INNER ** -0.5, 1.0, ((0, 8),)),
        "valve_leftside_array": bell_draw(key_of[20], (NETWORK_WIDTH * GATE_INNER,), NETWORK_WIDTH ** -0.5, 0.1875, ((0, 8),)),
        "valve_rightside_array": bell_draw(key_of[21], (GATE_INNER * NETWORK_WIDTH,), GATE_INNER ** -0.5, 0.5, ((0, 8),)),
        "erasure_lookup_stretch": jnp.clip(0.29882812 + 1.2011719 * jax.random.uniform(key_of[22], (NETWORK_WIDTH,), jnp.float32) ** levels(key_of[22], (NETWORK_WIDTH,), ((0, 8),), -0.2, 0.2), 0.29882812, 1.5).astype(jnp.bfloat16),
        "stored_lookup_speed": jnp.clip(0.19921875 + 1.5976562 * jax.random.uniform(key_of[23], (NETWORK_WIDTH,), jnp.float32) ** levels(key_of[23], (NETWORK_WIDTH,), ((0, 8),), -0.2, 0.2), 0.19921875, 1.796875).astype(jnp.bfloat16),
        "present_token_boost": bell_draw(key_of[24], (NETWORK_WIDTH,), 0.5, 3.0, ((0, 8),)),
        "cluster_norming_amplitude_array": jnp.clip(1.0 + 0.1 * jax.random.normal(key_of[25], (NETWORK_WIDTH,), jnp.float32), 0.5, 1.5).astype(jnp.bfloat16),
        "cluster_norming_offset_array": bell_draw(key_of[26], (NETWORK_WIDTH,), 0.3, 1.5, ((0, 8),)),
        "later_norming_amplitude_arg": jnp.clip(1.0 + 0.1 * jax.random.normal(key_of[27], (NETWORK_WIDTH,), jnp.float32), 0.5, 1.5).astype(jnp.bfloat16),
        "later_norming_offset_arg": bell_draw(key_of[28], (NETWORK_WIDTH,), 0.3, 1.5, ((0, 8),)),
        "feature_lag_blend": jnp.clip(1.0 * jax.random.uniform(key_of[29], (NETWORK_WIDTH,), jnp.float32) ** levels(key_of[29], (NETWORK_WIDTH,), ((0, 8),), -0.2, 0.2), 0.0, 1.0).astype(jnp.bfloat16),
        "perceptron_lookup_array": bell_draw(key_of[30], (NETWORK_WIDTH * FEEDFORWARD_UNITS,), NETWORK_WIDTH ** -0.5, 0.1875, ((0, 8),)),
        "perceptron_content_array": bell_draw(key_of[31], (FEEDFORWARD_UNITS * NETWORK_WIDTH,), FEEDFORWARD_UNITS ** -0.5, 0.09375, ((0, 8),)),
    }


@jax.custom_vjp
def lowrank_hidden(v):
    return lax.optimization_barrier(v.astype(jnp.bfloat16)).astype(jnp.float32)

@jax.custom_vjp
def low_back(v):
    return v

def low_keep(v):
    return (lowrank_hidden(v), None)

def low_pass(kept, grad):
    return (grad,)

def back_keep(v):
    return (v, None)

def back_low(kept, grad):
    return (lowrank_hidden(grad),)
lowrank_hidden.defvjp(low_keep, low_pass)
low_back.defvjp(back_keep, back_low)
HIGHEST = lax.Precision.HIGHEST
DECAY_FACTOR = 0.606531
CLUSTER_EPSILON = 0.00064
NORM_EPS = 1e-05

def layout():
    return ((NETWORK_WIDTH,), (NETWORK_WIDTH,), (6, NETWORK_WIDTH), (NETWORK_WIDTH, NETWORK_WIDTH), (NETWORK_WIDTH, NETWORK_WIDTH), (NETWORK_WIDTH, NETWORK_WIDTH), (NETWORK_WIDTH, NETWORK_WIDTH), (NETWORK_WIDTH,), (NETWORK_WIDTH, DECAY_INNER), (DECAY_INNER, NETWORK_WIDTH), (NETWORK_WIDTH,), (NETWORK_WIDTH, RATE_INNER), (RATE_INNER, NETWORK_WIDTH), (NETWORK_WIDTH,), (NETWORK_WIDTH, VALUE_RES_INNER), (VALUE_RES_INNER, NETWORK_WIDTH), (NETWORK_WIDTH, GATE_INNER), (GATE_INNER, NETWORK_WIDTH), (NETWORK_WIDTH,), (NETWORK_WIDTH,), (NETWORK_WIDTH,), (NETWORK_WIDTH,), (NETWORK_WIDTH,), (NETWORK_WIDTH,), (NETWORK_WIDTH,), (NETWORK_WIDTH,), (NETWORK_WIDTH, FEEDFORWARD_UNITS), (FEEDFORWARD_UNITS, NETWORK_WIDTH))

def layer_norm(values, scale_gain, shift_bias):
    average_level = values - lax.optimization_barrier(jnp.mean(values, axis=1, keepdims=True))
    variance_width = lax.optimization_barrier(jnp.mean(average_level * average_level, axis=1, keepdims=True))
    return average_level * lax.rsqrt(variance_width + NORM_EPS) * scale_gain + shift_bias

def prev_rows(values, edge_row, keeping):
    return jnp.concatenate([edge_row, values[:-1]], axis=0) * keeping[:, None]

def spread_mix(standardized_lines, before, mixing):
    delta = before - standardized_lines
    return tuple((standardized_lines + delta * mixing[number] for number in range(6)))

def channel_in(standardized_lines, before, mixing):
    return standardized_lines + (before - standardized_lines) * mixing

def prepare_inputs(acceptor_lines, key_projected_rows, unmixed_value_rows, decay_lowrank_output, value_residual_lowrank, rate_lowrank_output, initial_layer_value, fading_feature_odds, learning_speed_odds, content_skip_odds, erasure_lookup_stretch, stored_lookup_speed):
    decay_factors = jnp.exp(-DECAY_FACTOR * jax.nn.sigmoid(fading_feature_odds + decay_lowrank_output))
    content_outcome_lines = unmixed_value_rows + (initial_layer_value - unmixed_value_rows) * jax.nn.sigmoid(content_skip_odds + value_residual_lowrank)
    rate_sigmoid_gate = jax.nn.sigmoid(learning_speed_odds + rate_lowrank_output)
    head_shape = (acceptor_lines.shape[0], acceptor_lines.shape[1] // HEAD_SIZE, HEAD_SIZE)
    standardized_lines = (key_projected_rows * erasure_lookup_stretch).reshape(head_shape)
    standardized_lines = standardized_lines * lax.rsqrt(lax.optimization_barrier(jnp.sum(standardized_lines * standardized_lines, axis=2, keepdims=True)) + 1e-06)
    lagged_lookup_entry = key_projected_rows * (1.0 + (rate_sigmoid_gate - 1.0) * stored_lookup_speed)
    removal = standardized_lines * rate_sigmoid_gate.reshape(head_shape)
    return (acceptor_lines.reshape(head_shape), decay_factors.reshape(head_shape), lagged_lookup_entry.reshape(head_shape), content_outcome_lines.reshape(head_shape), standardized_lines, removal)

def complete_unit(unit_outcomes, acceptor_lines, lagged_lookup_entry, content_outcome_lines, valve_exit_lines, cluster_norming_amplitude_lines, cluster_norming_offset_lines, present_token_boost):
    average_level = unit_outcomes - lax.optimization_barrier(jnp.mean(unit_outcomes, axis=2, keepdims=True))
    variance_width = lax.optimization_barrier(jnp.mean(average_level * average_level, axis=2, keepdims=True))
    linear_extent = (unit_outcomes.shape[0], unit_outcomes.shape[1] * unit_outcomes.shape[2])
    standardized_lines = (average_level * lax.rsqrt(variance_width + CLUSTER_EPSILON)).reshape(linear_extent) * cluster_norming_amplitude_lines + cluster_norming_offset_lines
    boost_summed = lax.optimization_barrier(jnp.sum(acceptor_lines * lagged_lookup_entry * present_token_boost.reshape(unit_outcomes.shape[1:]), axis=2, keepdims=True))
    return (standardized_lines + (boost_summed * content_outcome_lines).reshape(linear_extent)) * valve_exit_lines

def state_step(current, inputs):
    acceptor_lines, decay_factors, keyed, content_outcome_lines, standardized_lines, removal, keeping = inputs
    current = current * keeping
    current = current * decay_factors[:, None, :] - lax.optimization_barrier(jnp.sum(current * standardized_lines[:, None, :], axis=2, keepdims=True)) * removal[:, None, :] + content_outcome_lines[:, :, None] * keyed[:, None, :]
    return (current, lax.optimization_barrier(jnp.sum(current * acceptor_lines[:, None, :], axis=2)))

def sweep_block(current, block_inputs):
    return lax.scan(state_step, current, block_inputs)

def recurrence(initial, inputs, keeping):
    length = keeping.shape[0]
    block_size = math.gcd(length, 64)
    blocks = length // block_size
    folded = tuple((tensor_entry.reshape((blocks, block_size) + tensor_entry.shape[1:]) for tensor_entry in inputs + (keeping,)))
    last_state, unit_outcomes = lax.scan(jax.checkpoint(sweep_block), initial, folded)
    return (unit_outcomes.reshape((length,) + unit_outcomes.shape[2:]), last_state)

def apply_projection(left_low, right):
    return low_back(jnp.dot(left_low, right, precision=HIGHEST))

def block_layer(block_rows, leading_rows, keeping, tensor_sequence):
    earlier_norming_amplitude, earlier_norming_offset, lagged_blend_lines, acceptor_array_formed, lookup_array_formed, content_array_formed, exit_array_formed, fading_odds_offset, fading_narrow_array, fading_widen_array, speed_odds_offset, speed_narrow_array, speed_widen_array, content_skip_odds_offset, content_skip_narrow_array, content_skip_widen_array, valve_narrow_array, valve_widen_array, unitnorm_erasure_lookup, speed_weighted_lookup, boost_blend, cluster_norming_amplitude_arg, cluster_norming_offset_arg, later_norming_amplitude, later_norming_offset, feature_blend_lines, latent_entry_array, latent_exit_array = tensor_sequence
    zero_row = jnp.zeros((1, block_rows.shape[1]), jnp.float32)
    normed_one = layer_norm(block_rows, earlier_norming_amplitude, earlier_norming_offset)
    before_one = prev_rows(normed_one, zero_row, keeping)
    mixed = spread_mix(normed_one, before_one, lagged_blend_lines)
    recept_in, decay_input_rows, key_in, value_input_rows, rate_input_rows, gate_in = tuple((lowrank_hidden(tensor_entry) for tensor_entry in mixed))
    acceptor_lines = apply_projection(recept_in, acceptor_array_formed)
    key_projected_rows = apply_projection(key_in, lookup_array_formed)
    unmixed_value_rows = apply_projection(value_input_rows, content_array_formed)
    decay_lowrank_output = apply_projection(lowrank_hidden(jnp.tanh(apply_projection(decay_input_rows, fading_narrow_array))), fading_widen_array)
    rate_lowrank_output = apply_projection(lowrank_hidden(apply_projection(rate_input_rows, speed_narrow_array)), speed_widen_array)
    value_residual_lowrank = apply_projection(lowrank_hidden(apply_projection(value_input_rows, content_skip_narrow_array)), content_skip_widen_array)
    valve_exit_lines = apply_projection(lowrank_hidden(jax.nn.sigmoid(apply_projection(gate_in, valve_narrow_array))), valve_widen_array)
    readied_arguments = prepare_inputs(acceptor_lines, key_projected_rows, unmixed_value_rows, decay_lowrank_output, value_residual_lowrank, rate_lowrank_output, leading_rows, fading_odds_offset, speed_odds_offset, content_skip_odds_offset, unitnorm_erasure_lookup, speed_weighted_lookup)
    head_count = block_rows.shape[1] // HEAD_SIZE
    zero_state = jnp.zeros((head_count, HEAD_SIZE, HEAD_SIZE), jnp.float32)
    unit_outcomes, last_state = recurrence(zero_state, readied_arguments, keeping)
    blended_outcome = complete_unit(unit_outcomes, readied_arguments[0], readied_arguments[2], readied_arguments[3], valve_exit_lines, cluster_norming_amplitude_arg, cluster_norming_offset_arg, boost_blend)
    residual_mid = block_rows + apply_projection(lowrank_hidden(blended_outcome), exit_array_formed)
    normed_two = layer_norm(residual_mid, later_norming_amplitude, later_norming_offset)
    before_two = prev_rows(normed_two, zero_row, keeping)
    channel = lowrank_hidden(channel_in(normed_two, before_two, feature_blend_lines))
    hidden = jnp.square(jax.nn.relu(apply_projection(channel, latent_entry_array)))
    return residual_mid + apply_projection(lowrank_hidden(hidden), latent_exit_array)

def reference(unit_entry_lines, opening_stratum_contents, packed_sequence_ids, unit_exit_slope, earlier_norming_amplitude_arg, earlier_norming_offset_arg, token_lag_blends, acceptor_mapping, lookup_mapping, content_mapping, exit_mapping, fading_feature_odds, fading_leftside_array, fading_rightside_array, learning_speed_odds, speed_leftside_array, speed_rightside_array, content_skip_odds, content_skip_leftside, content_skip_rightside, valve_leftside_array, valve_rightside_array, erasure_lookup_stretch, stored_lookup_speed, present_token_boost, cluster_norming_amplitude_array, cluster_norming_offset_array, later_norming_amplitude_arg, later_norming_offset_arg, feature_lag_blend, perceptron_lookup_array, perceptron_content_array):
    tensor_bundle = [tensor_entry.astype(jnp.float32) for tensor_entry in (earlier_norming_amplitude_arg, earlier_norming_offset_arg, token_lag_blends, acceptor_mapping, lookup_mapping, content_mapping, exit_mapping, fading_feature_odds, fading_leftside_array, fading_rightside_array, learning_speed_odds, speed_leftside_array, speed_rightside_array, content_skip_odds, content_skip_leftside, content_skip_rightside, valve_leftside_array, valve_rightside_array, erasure_lookup_stretch, stored_lookup_speed, present_token_boost, cluster_norming_amplitude_array, cluster_norming_offset_array, later_norming_amplitude_arg, later_norming_offset_arg, feature_lag_blend, perceptron_lookup_array, perceptron_content_array)]
    seg_before = jnp.concatenate([packed_sequence_ids[:1], packed_sequence_ids[:-1]])
    position = jnp.arange(TOKENS, dtype=jnp.int32) % SEQ
    keeping = jnp.where((position == 0) | (packed_sequence_ids != seg_before), 0.0, 1.0).astype(jnp.float32)
    sequences = TOKENS // SEQ

    def forward(block_rows, leading_rows, *tensor_sequence):
        shaped_params = tuple((tensor_entry.reshape(target) for tensor_entry, target in zip(tensor_sequence, layout())))

        def one_sequence(tensor_entry):
            return block_layer(tensor_entry[0], tensor_entry[1], tensor_entry[2], shaped_params)
        result = lax.map(jax.checkpoint(one_sequence), (block_rows.reshape(sequences, SEQ, NETWORK_WIDTH), leading_rows.reshape(sequences, SEQ, NETWORK_WIDTH), keeping.reshape(sequences, SEQ)))
        return result.reshape(TOKENS, NETWORK_WIDTH)
    block_out, pullback = jax.vjp(forward, unit_entry_lines.astype(jnp.float32), opening_stratum_contents.astype(jnp.float32), *tensor_bundle)
    gradients = pullback(unit_exit_slope.astype(jnp.float32))
    return (block_out.astype(jnp.bfloat16), gradients[0], gradients[1], gradients[2], gradients[3], gradients[4], gradients[5], gradients[6], gradients[7], gradients[8], gradients[9], gradients[10], gradients[11], gradients[12], gradients[13], gradients[14], gradients[15], gradients[16], gradients[17], gradients[18], gradients[19], gradients[20], gradients[21], gradients[22], gradients[23], gradients[24], gradients[25], gradients[26], gradients[27], gradients[28], gradients[29])
```

```python
import jax
import jax.numpy as jnp
from jax import lax
from jax.sharding import PartitionSpec as P

NETWORK_WIDTH = 1024
HEAD_SIZE = 64
FEEDFORWARD_UNITS = 4096
DECAY_INNER = 64
RATE_INNER = 64
VALUE_RES_INNER = 32
GATE_INNER = 160


HIGHEST = lax.Precision.HIGHEST
MATRIX_PRECISION = lax.Precision.HIGH
DECAY_FACTOR = 0.606531
CLUSTER_EPSILON = 0.00064
NORM_EPS = 1e-05


def shifted_2(block, axis, distance):
    devices = range(lax.axis_size(axis))
    route = [(i - distance, i) for i in devices if i - distance in devices]
    return lax.ppermute(block, axis, route)


BIG = (3, 4, 5, 6, 26, 27)


def chain_states(block_map, block_shift, axis):
    devices, mine = (lax.axis_size(axis), lax.axis_index(axis))
    pair = jnp.stack([block_map, block_shift]).astype(jnp.bfloat16)
    everything = lax.all_gather(pair, axis).astype(jnp.float32)
    maps = everything[:, 0]
    state = jnp.zeros_like(block_shift)
    for k in range(devices - 1):
        new = everything[k, 1]
        if k:
            new = new + jnp.einsum("hij,hjk->hik", state, maps[k], precision=HIGHEST)
        state = jnp.where(k < mine, new, state)
    return (maps, state)


def chain_grads(maps, local_grad, axis):
    devices, mine = (lax.axis_size(axis), lax.axis_index(axis))
    everything = lax.all_gather(local_grad.astype(jnp.bfloat16), axis).astype(jnp.float32)
    grad = jnp.zeros_like(local_grad)
    for k in range(devices - 1, 0, -1):
        new = everything[k]
        if k < devices - 1:
            new = new + jnp.einsum("hij,hlj->hil", grad, maps[k], precision=HIGHEST)
        grad = jnp.where(k > mine, new, grad)
    return grad


def gather_weights(shards):
    shapes = layout()
    small = [i for i in range(len(shards)) if i not in BIG]
    packed = lax.all_gather(jnp.concatenate([shards[i] for i in small]), "wa")
    whole = [None] * len(shards)
    at = 0
    for i in small:
        n = shards[i].shape[0]
        whole[i] = packed[:, at : at + n].reshape(shapes[i])
        at += n
    for i in BIG:
        whole[i] = lax.all_gather(shards[i].reshape(-1, shapes[i][1]), "wa", axis=0, tiled=True)
    return tuple(whole)


def reduce_big(grad):
    part = lax.psum_scatter(grad.astype(jnp.bfloat16), "wa", scatter_dimension=0, tiled=True)
    return lax.psum(part, "sa").reshape(-1).astype(jnp.float32)


def reduce_small(grads):
    owners = lax.axis_size("wa")
    packed = jnp.concatenate(
        [grad.astype(jnp.bfloat16).reshape(owners, -1) for grad in grads], axis=1
    )
    packed = jnp.pad(packed, ((0, 0), (0, -packed.shape[1] % 2048)))
    part = lax.psum_scatter(packed.reshape(-1, 128), "wa", scatter_dimension=0, tiled=True)
    total = lax.psum(part, "sa").reshape(-1).astype(jnp.float32)
    out = []
    at = 0
    for grad in grads:
        n = grad.size // owners
        out.append(total[at : at + n])
        at += n
    return out


def layout():
    return (
        (NETWORK_WIDTH,),
        (NETWORK_WIDTH,),
        (6, NETWORK_WIDTH),
        (NETWORK_WIDTH, NETWORK_WIDTH),
        (NETWORK_WIDTH, NETWORK_WIDTH),
        (NETWORK_WIDTH, NETWORK_WIDTH),
        (NETWORK_WIDTH, NETWORK_WIDTH),
        (NETWORK_WIDTH,),
        (NETWORK_WIDTH, DECAY_INNER),
        (DECAY_INNER, NETWORK_WIDTH),
        (NETWORK_WIDTH,),
        (NETWORK_WIDTH, RATE_INNER),
        (RATE_INNER, NETWORK_WIDTH),
        (NETWORK_WIDTH,),
        (NETWORK_WIDTH, VALUE_RES_INNER),
        (VALUE_RES_INNER, NETWORK_WIDTH),
        (NETWORK_WIDTH, GATE_INNER),
        (GATE_INNER, NETWORK_WIDTH),
        (NETWORK_WIDTH,),
        (NETWORK_WIDTH,),
        (NETWORK_WIDTH,),
        (NETWORK_WIDTH,),
        (NETWORK_WIDTH,),
        (NETWORK_WIDTH,),
        (NETWORK_WIDTH,),
        (NETWORK_WIDTH,),
        (NETWORK_WIDTH, FEEDFORWARD_UNITS),
        (FEEDFORWARD_UNITS, NETWORK_WIDTH),
    )


def matrices(tensor_bundle):
    return tuple(
        (tensor_bundle[number] for number in (3, 4, 5, 6, 8, 9, 11, 12, 14, 15, 16, 17, 26, 27))
    )


def layer_norm(values, scale_gain, shift_bias):
    average_level = values - jnp.mean(values, axis=1, keepdims=True)
    variance_width = jnp.mean(average_level * average_level, axis=1, keepdims=True)
    return average_level * lax.rsqrt(variance_width + NORM_EPS) * scale_gain + shift_bias


def prev_rows(values, edge_row, keeping):
    return jnp.concatenate([edge_row, values[:-1]], axis=0) * keeping[:, None]


def spread_mix(standardized_lines, before, mixing):
    delta = before - standardized_lines
    return tuple((standardized_lines + delta * mixing[number] for number in range(6)))


def channel_in(standardized_lines, before, mixing):
    return standardized_lines + (before - standardized_lines) * mixing


def prepare_inputs(
    acceptor_lines,
    key_projected_rows,
    unmixed_value_rows,
    decay_lowrank_output,
    value_residual_lowrank,
    rate_lowrank_output,
    initial_layer_value,
    fading_feature_odds,
    learning_speed_odds,
    content_skip_odds,
    erasure_lookup_stretch,
    stored_lookup_speed,
):
    log_decay = -DECAY_FACTOR * jax.nn.sigmoid(fading_feature_odds + decay_lowrank_output)
    content_outcome_lines = unmixed_value_rows + (
        initial_layer_value - unmixed_value_rows
    ) * jax.nn.sigmoid(content_skip_odds + value_residual_lowrank)
    rate_sigmoid_gate = jax.nn.sigmoid(learning_speed_odds + rate_lowrank_output)
    head_shape = (acceptor_lines.shape[0], acceptor_lines.shape[1] // HEAD_SIZE, HEAD_SIZE)
    standardized_lines = (key_projected_rows * erasure_lookup_stretch).reshape(head_shape)
    standardized_lines = standardized_lines * lax.rsqrt(
        jnp.sum(standardized_lines * standardized_lines, axis=2, keepdims=True) + 1e-06
    )
    lagged_lookup_entry = key_projected_rows * (
        1.0 + (rate_sigmoid_gate - 1.0) * stored_lookup_speed
    )
    removal = standardized_lines * rate_sigmoid_gate.reshape(head_shape)
    return (
        acceptor_lines.reshape(head_shape),
        log_decay.reshape(head_shape),
        lagged_lookup_entry.reshape(head_shape),
        content_outcome_lines.reshape(head_shape),
        standardized_lines,
        removal,
    )


def complete_unit(
    unit_outcomes,
    acceptor_lines,
    lagged_lookup_entry,
    content_outcome_lines,
    valve_exit_lines,
    cluster_norming_amplitude_lines,
    cluster_norming_offset_lines,
    present_token_boost,
):
    average_level = unit_outcomes - jnp.mean(unit_outcomes, axis=2, keepdims=True)
    variance_width = jnp.mean(average_level * average_level, axis=2, keepdims=True)
    linear_extent = (unit_outcomes.shape[0], unit_outcomes.shape[1] * unit_outcomes.shape[2])
    standardized_lines = (average_level * lax.rsqrt(variance_width + CLUSTER_EPSILON)).reshape(
        linear_extent
    ) * cluster_norming_amplitude_lines + cluster_norming_offset_lines
    boost_summed = jnp.sum(
        acceptor_lines * lagged_lookup_entry * present_token_boost.reshape(unit_outcomes.shape[1:]),
        axis=2,
        keepdims=True,
    )
    return (
        standardized_lines + (boost_summed * content_outcome_lines).reshape(linear_extent)
    ) * valve_exit_lines


def batched(spec, left, right):
    return jnp.einsum(spec, left, right, precision=MATRIX_PRECISION)


def unit_lower_inverse(low):
    size = low.shape[-1]
    rows = lax.broadcasted_iota(jnp.int32, (size, size), 0)
    cols = lax.broadcasted_iota(jnp.int32, (size, size), 1)

    def corner(span):
        return (rows // (2 * span) == cols // (2 * span)) & (rows // span > cols // span)

    found = jnp.where(rows == cols, 1.0, 0.0) - jnp.where(corner(1), low, 0.0)
    span = 2
    while span < size:
        below = jnp.where(corner(span), low, 0.0)
        found = found - batched("htm,hms->hts", batched("htm,hms->hts", found, below), found)
        span *= 2
    return found


@jax.custom_vjp
def triangle_solve(low, right):
    return batched("hts,hsj->htj", unit_lower_inverse(low), right)


def triangle_forward(low, right):
    inverse = unit_lower_inverse(low)
    solved = batched("hts,hsj->htj", inverse, right)
    return (solved, (inverse, solved))


def triangle_backward(kept, grad):
    inverse, solved = kept
    grad_right = batched("hts,htj->hsj", inverse, grad)
    return (-batched("htj,hsj->hts", grad_right, solved), grad_right)


triangle_solve.defvjp(triangle_forward, triangle_backward)


def block_sweep(recept, log_decay, keyed, valued, kappa, removal, keeping):
    length, width = (recept.shape[0], recept.shape[2])
    recept, log_decay, keyed, valued, kappa, removal = (
        jnp.swapaxes(part, 0, 1)
        for part in (recept, log_decay, keyed, valued, kappa, removal)
    )
    rows = lax.broadcasted_iota(jnp.int32, (length, length), 0)
    cols = lax.broadcasted_iota(jnp.int32, (length, length), 1)
    upto = jnp.where(cols <= rows, 1.0, 0.0)
    resets = jnp.sum(upto * (1.0 - keeping)[None, :], axis=1)
    same = resets[:, None] == resets[None, :]
    reached = jnp.where(resets == 0, 1.0, 0.0)[:, None]
    lasting = jnp.where(resets == resets[-1], 1.0, 0.0)[:, None]
    total = jnp.einsum("ts,hsj->htj", upto, log_decay, precision=HIGHEST)
    middle = lax.stop_gradient(total[:, length // 2 - 1 : length // 2])
    rising = jnp.exp(total - middle)
    queries = jnp.concatenate([kappa * jnp.exp(total - log_decay - middle), recept * rising], 1)
    falling = jnp.exp(middle - total)
    keys = jnp.concatenate([keyed * falling, removal * falling], 1)
    scores = batched("htj,hsj->hts", queries, keys)
    before = same & (cols < rows)
    until = same & (cols <= rows)
    write_to_kappa = jnp.where(before, scores[:, :length, :length], 0.0)
    erase_to_kappa = jnp.where(before, scores[:, :length, length:], 0.0)
    write_to_out = jnp.where(until, scores[:, length:, :length], 0.0)
    erase_to_out = jnp.where(until, scores[:, length:, length:], 0.0)
    entering_kappa = reached * kappa * jnp.exp(total - log_decay)
    entering_out = reached * recept * jnp.exp(total)
    solved = triangle_solve(
        erase_to_kappa,
        jnp.concatenate([entering_kappa, batched("hts,hsi->hti", write_to_kappa, valued)], 2),
    )
    erased = batched("hts,hsj->htj", erase_to_out, solved)
    carried = entering_out - erased[:, :, :width]
    local_out = batched("hts,hsi->hti", write_to_out, valued) - erased[:, :, width:]
    ending = lasting * jnp.exp(total[:, -1:] - total)
    erasing = batched("hsi,hsj->hij", solved, removal * ending)
    end_decay = reached[-1, 0] * jnp.exp(total[:, -1])
    span_map = jnp.eye(width, dtype=jnp.float32) * end_decay[:, None, :] - erasing[:, :width]
    span_shift = batched("hsi,hsj->hij", valued, keyed * ending) - erasing[:, width:]
    return (span_map, span_shift, local_out, carried)


def matrix_multiply(left, right):
    return jnp.dot(left, right, preferred_element_type=jnp.float32)


def matrix_product_pullback(grad_out, left_low, right):
    grad_low = grad_out.astype(jnp.bfloat16)
    grad_weight = lax.dot_general(
        left_low, grad_low, (((0,), (0,)), ((), ())), preferred_element_type=jnp.float32
    )
    grad_left = lax.dot_general(
        grad_low, right, (((1,), (1,)), ((), ())), preferred_element_type=jnp.float32
    )
    return (grad_left, grad_weight)


def body(
    unit_entry_lines,
    opening_stratum_contents,
    packed_sequence_ids,
    unit_exit_slope,
    earlier_norming_amplitude_arg,
    earlier_norming_offset_arg,
    token_lag_blends,
    acceptor_mapping,
    lookup_mapping,
    content_mapping,
    exit_mapping,
    fading_feature_odds,
    fading_leftside_array,
    fading_rightside_array,
    learning_speed_odds,
    speed_leftside_array,
    speed_rightside_array,
    content_skip_odds,
    content_skip_leftside,
    content_skip_rightside,
    valve_leftside_array,
    valve_rightside_array,
    erasure_lookup_stretch,
    stored_lookup_speed,
    present_token_boost,
    cluster_norming_amplitude_array,
    cluster_norming_offset_array,
    later_norming_amplitude_arg,
    later_norming_offset_arg,
    feature_lag_blend,
    perceptron_lookup_array,
    perceptron_content_array,
):
    shards = (
        earlier_norming_amplitude_arg,
        earlier_norming_offset_arg,
        token_lag_blends,
        acceptor_mapping,
        lookup_mapping,
        content_mapping,
        exit_mapping,
        fading_feature_odds,
        fading_leftside_array,
        fading_rightside_array,
        learning_speed_odds,
        speed_leftside_array,
        speed_rightside_array,
        content_skip_odds,
        content_skip_leftside,
        content_skip_rightside,
        valve_leftside_array,
        valve_rightside_array,
        erasure_lookup_stretch,
        stored_lookup_speed,
        present_token_boost,
        cluster_norming_amplitude_array,
        cluster_norming_offset_array,
        later_norming_amplitude_arg,
        later_norming_offset_arg,
        feature_lag_blend,
        perceptron_lookup_array,
        perceptron_content_array,
    )
    tensor_bundle = gather_weights(shards)
    small = [
        tensor_bundle[number].astype(jnp.float32)
        for number in (0, 1, 2, 7, 10, 13, 18, 19, 20, 21, 22, 23, 24, 25)
    ]
    (
        earlier_norming_amplitude,
        earlier_norming_offset,
        lagged_blend_lines,
        fading_odds_offset,
        speed_odds_offset,
        content_skip_odds_offset,
        unitnorm_erasure_lookup,
        speed_weighted_lookup,
        boost_blend,
        cluster_norming_amplitude_arg,
        cluster_norming_offset_arg,
        later_norming_amplitude,
        later_norming_offset,
        feature_blend_lines,
    ) = small
    (
        acceptor_array_formed,
        lookup_array_formed,
        content_array_formed,
        exit_array_formed,
        fading_narrow_array,
        fading_widen_array,
        speed_narrow_array,
        speed_widen_array,
        content_skip_narrow_array,
        content_skip_widen_array,
        valve_narrow_array,
        valve_widen_array,
        latent_entry_array,
        latent_exit_array,
    ) = matrices(tensor_bundle)
    length = unit_entry_lines.shape[0]
    model_width = unit_entry_lines.shape[1]
    residual_in = unit_entry_lines.astype(jnp.float32)
    initial_layer_value = opening_stratum_contents.astype(jnp.float32)
    normed_one, ln_one_back = jax.vjp(
        layer_norm, residual_in, earlier_norming_amplitude, earlier_norming_offset
    )
    edge_one, edge_segment = shifted_2(
        (normed_one[-1:], packed_sequence_ids[-1:].astype(jnp.float32)), "sa", 1
    )
    first_fresh = jnp.where(
        lax.axis_index("sa") == 0,
        1.0,
        jnp.where(packed_sequence_ids[0].astype(jnp.float32) != edge_segment[0], 1.0, 0.0),
    )
    fresh_rows = jnp.concatenate(
        [
            first_fresh[None].astype(jnp.float32),
            jnp.where(packed_sequence_ids[1:] != packed_sequence_ids[:-1], 1.0, 0.0).astype(
                jnp.float32
            ),
        ]
    )
    keeping = 1.0 - fresh_rows

    def shift_rows(row_block, edge_row):
        return prev_rows(row_block, edge_row, keeping)

    before_one, prev_one_back = jax.vjp(shift_rows, normed_one, edge_one)
    mixed, mix_back = jax.vjp(spread_mix, normed_one, before_one, lagged_blend_lines)
    recept_in, decay_input_rows, key_in, value_input_rows, rate_input_rows, gate_in = tuple(
        (tensor_entry.astype(jnp.bfloat16) for tensor_entry in mixed)
    )
    acceptor_lines = matrix_multiply(recept_in, acceptor_array_formed)
    key_projected_rows = matrix_multiply(key_in, lookup_array_formed)
    unmixed_value_rows = matrix_multiply(value_input_rows, content_array_formed)
    decay_hidden = jnp.tanh(matrix_multiply(decay_input_rows, fading_narrow_array))
    decay_lowrank_hidden = decay_hidden.astype(jnp.bfloat16)
    decay_lowrank_output = matrix_multiply(decay_lowrank_hidden, fading_widen_array)
    rate_hidden_rows = matrix_multiply(rate_input_rows, speed_narrow_array).astype(jnp.bfloat16)
    rate_lowrank_output = matrix_multiply(rate_hidden_rows, speed_widen_array)
    value_residual_hidden = matrix_multiply(value_input_rows, content_skip_narrow_array).astype(
        jnp.bfloat16
    )
    value_residual_lowrank = matrix_multiply(value_residual_hidden, content_skip_widen_array)
    gate_sig = jax.nn.sigmoid(matrix_multiply(gate_in, valve_narrow_array))
    gate_low = gate_sig.astype(jnp.bfloat16)
    valve_exit_lines = matrix_multiply(gate_low, valve_widen_array)
    readied_arguments, prepare_back = jax.vjp(
        prepare_inputs,
        acceptor_lines,
        key_projected_rows,
        unmixed_value_rows,
        decay_lowrank_output,
        value_residual_lowrank,
        rate_lowrank_output,
        initial_layer_value,
        fading_odds_offset,
        speed_odds_offset,
        content_skip_odds_offset,
        unitnorm_erasure_lookup,
        speed_weighted_lookup,
    )
    head_count = model_width // HEAD_SIZE

    def sweep(*parts):
        return block_sweep(*parts, keeping)

    (block_map, block_shift, local_out, carried), sweep_back = jax.vjp(sweep, *readied_arguments)
    block_maps, start_state = chain_states(block_map, block_shift, "sa")
    unit_outcomes = jnp.swapaxes(
        local_out + jnp.einsum("htj,hij->hti", carried, start_state, precision=HIGHEST), 0, 1
    )
    blended_outcome, finish_back = jax.vjp(
        complete_unit,
        unit_outcomes,
        readied_arguments[0],
        readied_arguments[2],
        readied_arguments[3],
        valve_exit_lines,
        cluster_norming_amplitude_arg,
        cluster_norming_offset_arg,
        boost_blend,
    )
    mixed_low = blended_outcome.astype(jnp.bfloat16)
    residual_mid = residual_in + matrix_multiply(mixed_low, exit_array_formed)
    normed_two, ln_two_back = jax.vjp(
        layer_norm, residual_mid, later_norming_amplitude, later_norming_offset
    )
    edge_two = shifted_2(normed_two[-1:], "sa", 1)
    before_two, prev_two_back = jax.vjp(shift_rows, normed_two, edge_two)
    channel, chan_back = jax.vjp(channel_in, normed_two, before_two, feature_blend_lines)
    channel_low = channel.astype(jnp.bfloat16)
    pre_act = matrix_multiply(channel_low, latent_entry_array)
    hidden_low = jnp.square(jax.nn.relu(pre_act)).astype(jnp.bfloat16)
    block_out = residual_mid + matrix_multiply(hidden_low, latent_exit_array)
    back_weights = matrices(tensor_bundle)
    (
        back_receptance,
        back_key,
        back_value,
        back_output,
        back_down_decay,
        pullback_up_decay,
        back_down_rate,
        pullback_up_rate,
        pullback_down_value_residual,
        pullback_up_value_residual,
        back_down_gate,
        back_up_gate,
        back_hidden_in,
        back_hidden_out,
    ) = back_weights
    grad_out = unit_exit_slope.astype(jnp.float32)
    grad_hidden, grad_ffn_value = matrix_product_pullback(grad_out, hidden_low, back_hidden_out)
    grad_pre = grad_hidden * 2.0 * jax.nn.relu(pre_act)
    grad_channel, grad_ffn_key = matrix_product_pullback(grad_pre, channel_low, back_hidden_in)
    grad_normed_two, grad_before_two, grad_mix_channel = chan_back(grad_channel)
    grad_rows_two, grad_edge_two = prev_two_back(grad_before_two)
    edge_back_two = shifted_2(grad_edge_two, "sa", -1)
    grad_normed_two = (
        grad_normed_two
        + grad_rows_two
        + jnp.concatenate(
            [jnp.zeros((length - 1, model_width), jnp.float32), edge_back_two], axis=0
        )
    )
    grad_mid, grad_ln2_gain, grad_ln2_bias = ln_two_back(grad_normed_two)
    grad_mid = grad_mid + grad_out
    grad_mixed, grad_w_output = matrix_product_pullback(grad_mid, mixed_low, back_output)
    (
        grad_outputs,
        grad_recept_a,
        grad_key_mixed_a,
        grad_valued_a,
        grad_gate_rows,
        grad_lnx_gain,
        grad_lnx_bias,
        present_token_boost_slope,
    ) = finish_back(grad_mixed)
    grad_heads = jnp.swapaxes(grad_outputs, 0, 1)
    local_grad = jnp.einsum("hti,htj->hij", grad_heads, carried, precision=HIGHEST)
    end_grad = chain_grads(block_maps, local_grad, "sa")
    state_grads = sweep_back(
        (
            jnp.einsum("hij,hil->hjl", start_state, end_grad, precision=HIGHEST),
            end_grad,
            grad_heads,
            jnp.einsum("hti,hij->htj", grad_heads, start_state, precision=HIGHEST),
        )
    )
    prep_grads = (
        state_grads[0] + grad_recept_a,
        state_grads[1],
        state_grads[2] + grad_key_mixed_a,
        state_grads[3] + grad_valued_a,
        state_grads[4],
        state_grads[5],
    )
    (
        grad_recept,
        grad_key_rows,
        grad_value_raw,
        decay_lowrank_output_gradient,
        value_residual_lowrank_gradient,
        rate_lowrank_output_gradient,
        grad_first,
        grad_decay_base,
        grad_rate_base,
        value_residual_logits_gradient,
        grad_key_norm,
        grad_key_rate,
    ) = prepare_back(prep_grads)
    grad_gate_low, grad_gate_up = matrix_product_pullback(grad_gate_rows, gate_low, back_up_gate)
    grad_gate_in, grad_gate_down = matrix_product_pullback(
        grad_gate_low * gate_sig * (1.0 - gate_sig), gate_in, back_down_gate
    )
    value_residual_hidden_gradient, value_residual_second_gradient = matrix_product_pullback(
        value_residual_lowrank_gradient, value_residual_hidden, pullback_up_value_residual
    )
    value_input_gradient_first, value_residual_first_gradient = matrix_product_pullback(
        value_residual_hidden_gradient, value_input_rows, pullback_down_value_residual
    )
    rate_hidden_gradient, rate_second_factor_gradient = matrix_product_pullback(
        rate_lowrank_output_gradient, rate_hidden_rows, pullback_up_rate
    )
    grad_rate_in, grad_rate_down = matrix_product_pullback(
        rate_hidden_gradient, rate_input_rows, back_down_rate
    )
    decay_lowrank_hidden_gradient, decay_second_factor_gradient = matrix_product_pullback(
        decay_lowrank_output_gradient, decay_lowrank_hidden, pullback_up_decay
    )
    grad_decay_in, grad_decay_down = matrix_product_pullback(
        decay_lowrank_hidden_gradient * (1.0 - decay_hidden * decay_hidden),
        decay_input_rows,
        back_down_decay,
    )
    grad_recept_in, grad_w_receptance = matrix_product_pullback(
        grad_recept, recept_in, back_receptance
    )
    grad_key_in, grad_w_key = matrix_product_pullback(grad_key_rows, key_in, back_key)
    grad_value_in_b, grad_w_value = matrix_product_pullback(
        grad_value_raw, value_input_rows, back_value
    )
    grad_normed_one, grad_before_one, grad_mix_time = mix_back(
        (
            grad_recept_in,
            grad_decay_in,
            grad_key_in,
            value_input_gradient_first + grad_value_in_b,
            grad_rate_in,
            grad_gate_in,
        )
    )
    grad_rows_one, grad_edge_one = prev_one_back(grad_before_one)
    edge_back_one = shifted_2(grad_edge_one, "sa", -1)
    grad_normed_one = (
        grad_normed_one
        + grad_rows_one
        + jnp.concatenate(
            [jnp.zeros((length - 1, model_width), jnp.float32), edge_back_one], axis=0
        )
    )
    grad_input, grad_ln1_gain, grad_ln1_bias = ln_one_back(grad_normed_one)
    grad_input = grad_input + grad_mid
    grads = (
        grad_ln1_gain,
        grad_ln1_bias,
        grad_mix_time,
        grad_w_receptance,
        grad_w_key,
        grad_w_value,
        grad_w_output,
        grad_decay_base,
        grad_decay_down,
        decay_second_factor_gradient,
        grad_rate_base,
        grad_rate_down,
        rate_second_factor_gradient,
        value_residual_logits_gradient,
        value_residual_first_gradient,
        value_residual_second_gradient,
        grad_gate_down,
        grad_gate_up,
        grad_key_norm,
        grad_key_rate,
        present_token_boost_slope,
        grad_lnx_gain,
        grad_lnx_bias,
        grad_ln2_gain,
        grad_ln2_bias,
        grad_mix_channel,
        grad_ffn_key,
        grad_ffn_value,
    )
    small_places = [i for i in range(len(grads)) if i not in BIG]
    summed = dict(zip(small_places, reduce_small([grads[i] for i in small_places])))
    for i in BIG:
        summed[i] = reduce_big(grads[i])
    summed = tuple((summed[i] for i in range(len(grads))))
    return (block_out.astype(jnp.bfloat16), grad_input, grad_first) + summed


def solution(mesh):
    return jax.shard_map(
        body,
        mesh=mesh,
        in_specs=(
            P(("wa", "sa"), None),
            P(("wa", "sa"), None),
            P(("wa", "sa")),
            P(("wa", "sa"), None),
            P("wa"),
            P("wa"),
            P("wa"),
            P("wa"),
            P("wa"),
            P("wa"),
            P("wa"),
            P("wa"),
            P("wa"),
            P("wa"),
            P("wa"),
            P("wa"),
            P("wa"),
            P("wa"),
            P("wa"),
            P("wa"),
            P("wa"),
            P("wa"),
            P("wa"),
            P("wa"),
            P("wa"),
            P("wa"),
            P("wa"),
            P("wa"),
            P("wa"),
            P("wa"),
            P("wa"),
            P("wa"),
        ),
        out_specs=(
            P(("wa", "sa"), None),
            P(("wa", "sa"), None),
            P(("wa", "sa"), None),
            P("wa"),
            P("wa"),
            P("wa"),
            P("wa"),
            P("wa"),
            P("wa"),
            P("wa"),
            P("wa"),
            P("wa"),
            P("wa"),
            P("wa"),
            P("wa"),
            P("wa"),
            P("wa"),
            P("wa"),
            P("wa"),
            P("wa"),
            P("wa"),
            P("wa"),
            P("wa"),
            P("wa"),
            P("wa"),
            P("wa"),
            P("wa"),
            P("wa"),
            P("wa"),
            P("wa"),
            P("wa"),
        ),
        check_vma=False,
    )
```

```python
import jax
import jax.numpy as jnp
from jax import lax
from jax.sharding import PartitionSpec as P

NETWORK_WIDTH = 1024
HEAD_SIZE = 64
FEEDFORWARD_UNITS = 4096
DECAY_INNER = 64
RATE_INNER = 64
VALUE_RES_INNER = 32
GATE_INNER = 160


HIGHEST = lax.Precision.HIGHEST
MATRIX_PRECISION = lax.Precision.HIGH
DECAY_FACTOR = 0.606531
CLUSTER_EPSILON = 0.00064
NORM_EPS = 1e-05


def shifted_2(block, axis, distance):
    devices = range(lax.axis_size(axis))
    route = [(i - distance, i) for i in devices if i - distance in devices]
    return lax.ppermute(block, axis, route)


SQUARE = (3, 4, 5, 6)
BIG = SQUARE + (26, 27)


def chain_states(block_map, block_shift, axis):
    devices, mine = (lax.axis_size(axis), lax.axis_index(axis))
    pair = jnp.stack([block_map, block_shift]).astype(jnp.bfloat16)
    everything = lax.all_gather(pair, axis).astype(jnp.float32)
    maps = everything[:, 0]
    state = jnp.zeros_like(block_shift)
    for k in range(devices - 1):
        new = everything[k, 1]
        if k:
            new = new + jnp.einsum("hij,hjk->hik", state, maps[k], precision=HIGHEST)
        state = jnp.where(k < mine, new, state)
    return (maps, state)


def chain_grads(maps, local_grad, axis):
    devices, mine = (lax.axis_size(axis), lax.axis_index(axis))
    everything = lax.all_gather(local_grad.astype(jnp.bfloat16), axis).astype(jnp.float32)
    grad = jnp.zeros_like(local_grad)
    for k in range(devices - 1, 0, -1):
        new = everything[k]
        if k < devices - 1:
            new = new + jnp.einsum("hij,hlj->hil", grad, maps[k], precision=HIGHEST)
        grad = jnp.where(k > mine, new, grad)
    return grad


def small_rows(flat, rows):
    flat = jnp.pad(flat, ((0, 0), (0, -flat.shape[1] % (rows * 128))))
    return flat.reshape(flat.shape[0] * rows, -1)


def gather_weights(shards):
    shapes = layout()
    small = [i for i in range(len(shards)) if i not in BIG]
    squares = [shards[i].reshape(-1, shapes[i][1]) for i in SQUARE]
    flat = small_rows(jnp.concatenate([shards[i] for i in small])[None], squares[0].shape[0])
    packed = lax.all_gather(jnp.concatenate(squares + [flat], 1), "wa", axis=0, tiled=True)
    whole = [None] * len(shards)
    at = 0
    for i in SQUARE:
        whole[i] = packed[:, at : at + shapes[i][1]]
        at += shapes[i][1]
    packed = packed[:, at:].reshape(lax.axis_size("wa"), -1)
    at = 0
    for i in small:
        n = shards[i].shape[0]
        whole[i] = packed[:, at : at + n].reshape(shapes[i])
        at += n
    for i in (26, 27):
        whole[i] = lax.all_gather(shards[i].reshape(-1, shapes[i][1]), "wa", axis=0, tiled=True)
    return tuple(whole)


def scattered(grad):
    return lax.psum_scatter(grad.astype(jnp.bfloat16), "wa", scatter_dimension=0, tiled=True)


def layout():
    return (
        (NETWORK_WIDTH,),
        (NETWORK_WIDTH,),
        (6, NETWORK_WIDTH),
        (NETWORK_WIDTH, NETWORK_WIDTH),
        (NETWORK_WIDTH, NETWORK_WIDTH),
        (NETWORK_WIDTH, NETWORK_WIDTH),
        (NETWORK_WIDTH, NETWORK_WIDTH),
        (NETWORK_WIDTH,),
        (NETWORK_WIDTH, DECAY_INNER),
        (DECAY_INNER, NETWORK_WIDTH),
        (NETWORK_WIDTH,),
        (NETWORK_WIDTH, RATE_INNER),
        (RATE_INNER, NETWORK_WIDTH),
        (NETWORK_WIDTH,),
        (NETWORK_WIDTH, VALUE_RES_INNER),
        (VALUE_RES_INNER, NETWORK_WIDTH),
        (NETWORK_WIDTH, GATE_INNER),
        (GATE_INNER, NETWORK_WIDTH),
        (NETWORK_WIDTH,),
        (NETWORK_WIDTH,),
        (NETWORK_WIDTH,),
        (NETWORK_WIDTH,),
        (NETWORK_WIDTH,),
        (NETWORK_WIDTH,),
        (NETWORK_WIDTH,),
        (NETWORK_WIDTH,),
        (NETWORK_WIDTH, FEEDFORWARD_UNITS),
        (FEEDFORWARD_UNITS, NETWORK_WIDTH),
    )


def matrices(tensor_bundle):
    return tuple(
        (tensor_bundle[number] for number in (3, 4, 5, 6, 8, 9, 11, 12, 14, 15, 16, 17, 26, 27))
    )


def layer_norm(values, scale_gain, shift_bias):
    average_level = values - jnp.mean(values, axis=1, keepdims=True)
    variance_width = jnp.mean(average_level * average_level, axis=1, keepdims=True)
    return average_level * lax.rsqrt(variance_width + NORM_EPS) * scale_gain + shift_bias


def prev_rows(values, edge_row, keeping):
    return jnp.concatenate([edge_row, values[:-1]], axis=0) * keeping[:, None]


def spread_mix(standardized_lines, before, mixing):
    delta = before - standardized_lines
    return tuple((standardized_lines + delta * mixing[number] for number in range(6)))


def channel_in(standardized_lines, before, mixing):
    return standardized_lines + (before - standardized_lines) * mixing


def prepare_inputs(
    acceptor_lines,
    key_projected_rows,
    unmixed_value_rows,
    decay_lowrank_output,
    value_residual_lowrank,
    rate_lowrank_output,
    initial_layer_value,
    fading_feature_odds,
    learning_speed_odds,
    content_skip_odds,
    erasure_lookup_stretch,
    stored_lookup_speed,
):
    log_decay = -DECAY_FACTOR * jax.nn.sigmoid(fading_feature_odds + decay_lowrank_output)
    content_outcome_lines = unmixed_value_rows + (
        initial_layer_value - unmixed_value_rows
    ) * jax.nn.sigmoid(content_skip_odds + value_residual_lowrank)
    rate_sigmoid_gate = jax.nn.sigmoid(learning_speed_odds + rate_lowrank_output)
    head_shape = (acceptor_lines.shape[0], acceptor_lines.shape[1] // HEAD_SIZE, HEAD_SIZE)
    standardized_lines = (key_projected_rows * erasure_lookup_stretch).reshape(head_shape)
    standardized_lines = standardized_lines * lax.rsqrt(
        jnp.sum(standardized_lines * standardized_lines, axis=2, keepdims=True) + 1e-06
    )
    lagged_lookup_entry = key_projected_rows * (
        1.0 + (rate_sigmoid_gate - 1.0) * stored_lookup_speed
    )
    removal = standardized_lines * rate_sigmoid_gate.reshape(head_shape)
    return (
        acceptor_lines.reshape(head_shape),
        log_decay.reshape(head_shape),
        lagged_lookup_entry.reshape(head_shape),
        content_outcome_lines.reshape(head_shape),
        standardized_lines,
        removal,
    )


def complete_unit(
    unit_outcomes,
    acceptor_lines,
    lagged_lookup_entry,
    content_outcome_lines,
    valve_exit_lines,
    cluster_norming_amplitude_lines,
    cluster_norming_offset_lines,
    present_token_boost,
):
    average_level = unit_outcomes - jnp.mean(unit_outcomes, axis=2, keepdims=True)
    variance_width = jnp.mean(average_level * average_level, axis=2, keepdims=True)
    linear_extent = (unit_outcomes.shape[0], unit_outcomes.shape[1] * unit_outcomes.shape[2])
    standardized_lines = (average_level * lax.rsqrt(variance_width + CLUSTER_EPSILON)).reshape(
        linear_extent
    ) * cluster_norming_amplitude_lines + cluster_norming_offset_lines
    boost_summed = jnp.sum(
        acceptor_lines * lagged_lookup_entry * present_token_boost.reshape(unit_outcomes.shape[1:]),
        axis=2,
        keepdims=True,
    )
    return (
        standardized_lines + (boost_summed * content_outcome_lines).reshape(linear_extent)
    ) * valve_exit_lines


def batched(spec, left, right):
    return jnp.einsum(spec, left, right, precision=MATRIX_PRECISION)


def unit_lower_inverse(low):
    size = low.shape[-1]
    rows = lax.broadcasted_iota(jnp.int32, (size, size), 0)
    cols = lax.broadcasted_iota(jnp.int32, (size, size), 1)

    def corner(span):
        return (rows // (2 * span) == cols // (2 * span)) & (rows // span > cols // span)

    found = jnp.where(rows == cols, 1.0, 0.0) - jnp.where(corner(1), low, 0.0)
    span = 2
    while span < size:
        below = jnp.where(corner(span), low, 0.0)
        found = found - batched("htm,hms->hts", batched("htm,hms->hts", found, below), found)
        span *= 2
    return found


@jax.custom_vjp
def triangle_solve(low, right):
    return batched("hts,hsj->htj", unit_lower_inverse(low), right)


def triangle_forward(low, right):
    inverse = unit_lower_inverse(low)
    solved = batched("hts,hsj->htj", inverse, right)
    return (solved, (inverse, solved))


def triangle_backward(kept, grad):
    inverse, solved = kept
    grad_right = batched("hts,htj->hsj", inverse, grad)
    return (-batched("htj,hsj->hts", grad_right, solved), grad_right)


triangle_solve.defvjp(triangle_forward, triangle_backward)


def block_sweep(recept, log_decay, keyed, valued, kappa, removal, keeping):
    length, width = (recept.shape[0], recept.shape[2])
    recept, log_decay, keyed, valued, kappa, removal = (
        jnp.swapaxes(part, 0, 1)
        for part in (recept, log_decay, keyed, valued, kappa, removal)
    )
    rows = lax.broadcasted_iota(jnp.int32, (length, length), 0)
    cols = lax.broadcasted_iota(jnp.int32, (length, length), 1)
    upto = jnp.where(cols <= rows, 1.0, 0.0)
    resets = jnp.sum(upto * (1.0 - keeping)[None, :], axis=1)
    same = resets[:, None] == resets[None, :]
    reached = jnp.where(resets == 0, 1.0, 0.0)[:, None]
    lasting = jnp.where(resets == resets[-1], 1.0, 0.0)[:, None]
    total = jnp.einsum("ts,hsj->htj", upto, log_decay, precision=HIGHEST)
    middle = lax.stop_gradient(total[:, length // 2 - 1 : length // 2])
    rising = jnp.exp(total - middle)
    queries = jnp.concatenate([kappa * jnp.exp(total - log_decay - middle), recept * rising], 1)
    falling = jnp.exp(middle - total)
    keys = jnp.concatenate([keyed * falling, removal * falling], 1)
    scores = batched("htj,hsj->hts", queries, keys)
    before = same & (cols < rows)
    until = same & (cols <= rows)
    write_to_kappa = jnp.where(before, scores[:, :length, :length], 0.0)
    erase_to_kappa = jnp.where(before, scores[:, :length, length:], 0.0)
    write_to_out = jnp.where(until, scores[:, length:, :length], 0.0)
    erase_to_out = jnp.where(until, scores[:, length:, length:], 0.0)
    entering_kappa = reached * kappa * jnp.exp(total - log_decay)
    entering_out = reached * recept * jnp.exp(total)
    solved = triangle_solve(
        erase_to_kappa,
        jnp.concatenate([entering_kappa, batched("hts,hsi->hti", write_to_kappa, valued)], 2),
    )
    erased = batched("hts,hsj->htj", erase_to_out, solved)
    carried = entering_out - erased[:, :, :width]
    local_out = batched("hts,hsi->hti", write_to_out, valued) - erased[:, :, width:]
    ending = lasting * jnp.exp(total[:, -1:] - total)
    erasing = batched("hsi,hsj->hij", solved, removal * ending)
    end_decay = reached[-1, 0] * jnp.exp(total[:, -1])
    span_map = jnp.eye(width, dtype=jnp.float32) * end_decay[:, None, :] - erasing[:, :width]
    span_shift = batched("hsi,hsj->hij", valued, keyed * ending) - erasing[:, width:]
    return (span_map, span_shift, local_out, carried)


def matrix_multiply(left, right):
    return jnp.dot(left, right, preferred_element_type=jnp.float32)


def matrix_product_pullback(grad_out, left_low, right):
    grad_low = grad_out.astype(jnp.bfloat16)
    grad_weight = lax.dot_general(
        left_low, grad_low, (((0,), (0,)), ((), ())), preferred_element_type=jnp.float32
    )
    grad_left = lax.dot_general(
        grad_low, right, (((1,), (1,)), ((), ())), preferred_element_type=jnp.float32
    )
    return (grad_left, grad_weight)


def body(
    unit_entry_lines,
    opening_stratum_contents,
    packed_sequence_ids,
    unit_exit_slope,
    earlier_norming_amplitude_arg,
    earlier_norming_offset_arg,
    token_lag_blends,
    acceptor_mapping,
    lookup_mapping,
    content_mapping,
    exit_mapping,
    fading_feature_odds,
    fading_leftside_array,
    fading_rightside_array,
    learning_speed_odds,
    speed_leftside_array,
    speed_rightside_array,
    content_skip_odds,
    content_skip_leftside,
    content_skip_rightside,
    valve_leftside_array,
    valve_rightside_array,
    erasure_lookup_stretch,
    stored_lookup_speed,
    present_token_boost,
    cluster_norming_amplitude_array,
    cluster_norming_offset_array,
    later_norming_amplitude_arg,
    later_norming_offset_arg,
    feature_lag_blend,
    perceptron_lookup_array,
    perceptron_content_array,
):
    shards = (
        earlier_norming_amplitude_arg,
        earlier_norming_offset_arg,
        token_lag_blends,
        acceptor_mapping,
        lookup_mapping,
        content_mapping,
        exit_mapping,
        fading_feature_odds,
        fading_leftside_array,
        fading_rightside_array,
        learning_speed_odds,
        speed_leftside_array,
        speed_rightside_array,
        content_skip_odds,
        content_skip_leftside,
        content_skip_rightside,
        valve_leftside_array,
        valve_rightside_array,
        erasure_lookup_stretch,
        stored_lookup_speed,
        present_token_boost,
        cluster_norming_amplitude_array,
        cluster_norming_offset_array,
        later_norming_amplitude_arg,
        later_norming_offset_arg,
        feature_lag_blend,
        perceptron_lookup_array,
        perceptron_content_array,
    )
    tensor_bundle = gather_weights(shards)
    small = [
        tensor_bundle[number].astype(jnp.float32)
        for number in (0, 1, 2, 7, 10, 13, 18, 19, 20, 21, 22, 23, 24, 25)
    ]
    (
        earlier_norming_amplitude,
        earlier_norming_offset,
        lagged_blend_lines,
        fading_odds_offset,
        speed_odds_offset,
        content_skip_odds_offset,
        unitnorm_erasure_lookup,
        speed_weighted_lookup,
        boost_blend,
        cluster_norming_amplitude_arg,
        cluster_norming_offset_arg,
        later_norming_amplitude,
        later_norming_offset,
        feature_blend_lines,
    ) = small
    (
        acceptor_array_formed,
        lookup_array_formed,
        content_array_formed,
        exit_array_formed,
        fading_narrow_array,
        fading_widen_array,
        speed_narrow_array,
        speed_widen_array,
        content_skip_narrow_array,
        content_skip_widen_array,
        valve_narrow_array,
        valve_widen_array,
        latent_entry_array,
        latent_exit_array,
    ) = matrices(tensor_bundle)
    length = unit_entry_lines.shape[0]
    model_width = unit_entry_lines.shape[1]
    residual_in = unit_entry_lines.astype(jnp.float32)
    initial_layer_value = opening_stratum_contents.astype(jnp.float32)
    normed_one, ln_one_back = jax.vjp(
        layer_norm, residual_in, earlier_norming_amplitude, earlier_norming_offset
    )
    edge_one, edge_segment = shifted_2(
        (normed_one[-1:], packed_sequence_ids[-1:].astype(jnp.float32)), "sa", 1
    )
    first_fresh = jnp.where(
        lax.axis_index("sa") == 0,
        1.0,
        jnp.where(packed_sequence_ids[0].astype(jnp.float32) != edge_segment[0], 1.0, 0.0),
    )
    fresh_rows = jnp.concatenate(
        [
            first_fresh[None].astype(jnp.float32),
            jnp.where(packed_sequence_ids[1:] != packed_sequence_ids[:-1], 1.0, 0.0).astype(
                jnp.float32
            ),
        ]
    )
    keeping = 1.0 - fresh_rows

    def shift_rows(row_block, edge_row):
        return prev_rows(row_block, edge_row, keeping)

    before_one, prev_one_back = jax.vjp(shift_rows, normed_one, edge_one)
    mixed, mix_back = jax.vjp(spread_mix, normed_one, before_one, lagged_blend_lines)
    recept_in, decay_input_rows, key_in, value_input_rows, rate_input_rows, gate_in = tuple(
        (tensor_entry.astype(jnp.bfloat16) for tensor_entry in mixed)
    )
    acceptor_lines = matrix_multiply(recept_in, acceptor_array_formed)
    key_projected_rows = matrix_multiply(key_in, lookup_array_formed)
    unmixed_value_rows = matrix_multiply(value_input_rows, content_array_formed)
    decay_hidden = jnp.tanh(matrix_multiply(decay_input_rows, fading_narrow_array))
    decay_lowrank_hidden = decay_hidden.astype(jnp.bfloat16)
    decay_lowrank_output = matrix_multiply(decay_lowrank_hidden, fading_widen_array)
    rate_hidden_rows = matrix_multiply(rate_input_rows, speed_narrow_array).astype(jnp.bfloat16)
    rate_lowrank_output = matrix_multiply(rate_hidden_rows, speed_widen_array)
    value_residual_hidden = matrix_multiply(value_input_rows, content_skip_narrow_array).astype(
        jnp.bfloat16
    )
    value_residual_lowrank = matrix_multiply(value_residual_hidden, content_skip_widen_array)
    gate_sig = jax.nn.sigmoid(matrix_multiply(gate_in, valve_narrow_array))
    gate_low = gate_sig.astype(jnp.bfloat16)
    valve_exit_lines = matrix_multiply(gate_low, valve_widen_array)
    readied_arguments, prepare_back = jax.vjp(
        prepare_inputs,
        acceptor_lines,
        key_projected_rows,
        unmixed_value_rows,
        decay_lowrank_output,
        value_residual_lowrank,
        rate_lowrank_output,
        initial_layer_value,
        fading_odds_offset,
        speed_odds_offset,
        content_skip_odds_offset,
        unitnorm_erasure_lookup,
        speed_weighted_lookup,
    )
    head_count = model_width // HEAD_SIZE

    def sweep(*parts):
        return block_sweep(*parts, keeping)

    (block_map, block_shift, local_out, carried), sweep_back = jax.vjp(sweep, *readied_arguments)
    block_map, block_shift, latent_entry_array = lax.optimization_barrier(
        (block_map, block_shift, latent_entry_array)
    )
    block_maps, start_state = chain_states(block_map, block_shift, "sa")
    unit_outcomes = jnp.swapaxes(
        local_out + jnp.einsum("htj,hij->hti", carried, start_state, precision=HIGHEST), 0, 1
    )
    blended_outcome, finish_back = jax.vjp(
        complete_unit,
        unit_outcomes,
        readied_arguments[0],
        readied_arguments[2],
        readied_arguments[3],
        valve_exit_lines,
        cluster_norming_amplitude_arg,
        cluster_norming_offset_arg,
        boost_blend,
    )
    mixed_low = blended_outcome.astype(jnp.bfloat16)
    residual_mid = residual_in + matrix_multiply(mixed_low, exit_array_formed)
    normed_two, ln_two_back = jax.vjp(
        layer_norm, residual_mid, later_norming_amplitude, later_norming_offset
    )
    edge_two = shifted_2(normed_two[-1:], "sa", 1)
    before_two, prev_two_back = jax.vjp(shift_rows, normed_two, edge_two)
    channel, chan_back = jax.vjp(channel_in, normed_two, before_two, feature_blend_lines)
    channel_low = channel.astype(jnp.bfloat16)
    pre_act = matrix_multiply(channel_low, latent_entry_array)
    hidden_low = jnp.square(jax.nn.relu(pre_act)).astype(jnp.bfloat16)
    block_out = residual_mid + matrix_multiply(hidden_low, latent_exit_array)
    back_weights = matrices(tensor_bundle)[:-2] + (latent_entry_array, latent_exit_array)
    (
        back_receptance,
        back_key,
        back_value,
        back_output,
        back_down_decay,
        pullback_up_decay,
        back_down_rate,
        pullback_up_rate,
        pullback_down_value_residual,
        pullback_up_value_residual,
        back_down_gate,
        back_up_gate,
        back_hidden_in,
        back_hidden_out,
    ) = back_weights
    grad_out = unit_exit_slope.astype(jnp.float32)
    grad_hidden, grad_ffn_value = matrix_product_pullback(grad_out, hidden_low, back_hidden_out)
    grad_pre = grad_hidden * 2.0 * jax.nn.relu(pre_act)
    grad_channel, grad_ffn_key = matrix_product_pullback(grad_pre, channel_low, back_hidden_in)
    grad_normed_two, grad_before_two, grad_mix_channel = chan_back(grad_channel)
    grad_rows_two, grad_edge_two = prev_two_back(grad_before_two)
    edge_back_two = shifted_2(grad_edge_two, "sa", -1)
    grad_normed_two = (
        grad_normed_two
        + grad_rows_two
        + jnp.concatenate(
            [jnp.zeros((length - 1, model_width), jnp.float32), edge_back_two], axis=0
        )
    )
    grad_mid, grad_ln2_gain, grad_ln2_bias = ln_two_back(grad_normed_two)
    grad_mid = grad_mid + grad_out
    grad_mixed, grad_w_output = matrix_product_pullback(grad_mid, mixed_low, back_output)
    (
        grad_outputs,
        grad_recept_a,
        grad_key_mixed_a,
        grad_valued_a,
        grad_gate_rows,
        grad_lnx_gain,
        grad_lnx_bias,
        present_token_boost_slope,
    ) = finish_back(grad_mixed)
    grad_heads = jnp.swapaxes(grad_outputs, 0, 1)
    local_grad = jnp.einsum("hti,htj->hij", grad_heads, carried, precision=HIGHEST)
    end_grad = chain_grads(block_maps, local_grad, "sa")
    state_grads = sweep_back(
        (
            jnp.einsum("hij,hil->hjl", start_state, end_grad, precision=HIGHEST),
            end_grad,
            grad_heads,
            jnp.einsum("hti,hij->htj", grad_heads, start_state, precision=HIGHEST),
        )
    )
    state_grads, value_part = lax.optimization_barrier((state_grads, scattered(grad_ffn_value)))
    key_part = scattered(grad_ffn_key)
    prep_grads = (
        state_grads[0] + grad_recept_a,
        state_grads[1],
        state_grads[2] + grad_key_mixed_a,
        state_grads[3] + grad_valued_a,
        state_grads[4],
        state_grads[5],
    )
    (
        grad_recept,
        grad_key_rows,
        grad_value_raw,
        decay_lowrank_output_gradient,
        value_residual_lowrank_gradient,
        rate_lowrank_output_gradient,
        grad_first,
        grad_decay_base,
        grad_rate_base,
        value_residual_logits_gradient,
        grad_key_norm,
        grad_key_rate,
    ) = prepare_back(prep_grads)
    grad_gate_low, grad_gate_up = matrix_product_pullback(grad_gate_rows, gate_low, back_up_gate)
    grad_gate_in, grad_gate_down = matrix_product_pullback(
        grad_gate_low * gate_sig * (1.0 - gate_sig), gate_in, back_down_gate
    )
    value_residual_hidden_gradient, value_residual_second_gradient = matrix_product_pullback(
        value_residual_lowrank_gradient, value_residual_hidden, pullback_up_value_residual
    )
    value_input_gradient_first, value_residual_first_gradient = matrix_product_pullback(
        value_residual_hidden_gradient, value_input_rows, pullback_down_value_residual
    )
    rate_hidden_gradient, rate_second_factor_gradient = matrix_product_pullback(
        rate_lowrank_output_gradient, rate_hidden_rows, pullback_up_rate
    )
    grad_rate_in, grad_rate_down = matrix_product_pullback(
        rate_hidden_gradient, rate_input_rows, back_down_rate
    )
    decay_lowrank_hidden_gradient, decay_second_factor_gradient = matrix_product_pullback(
        decay_lowrank_output_gradient, decay_lowrank_hidden, pullback_up_decay
    )
    grad_decay_in, grad_decay_down = matrix_product_pullback(
        decay_lowrank_hidden_gradient * (1.0 - decay_hidden * decay_hidden),
        decay_input_rows,
        back_down_decay,
    )
    grad_recept_in, grad_w_receptance = matrix_product_pullback(
        grad_recept, recept_in, back_receptance
    )
    grad_key_in, grad_w_key = matrix_product_pullback(grad_key_rows, key_in, back_key)
    grad_value_in_b, grad_w_value = matrix_product_pullback(
        grad_value_raw, value_input_rows, back_value
    )
    grad_normed_one, grad_before_one, grad_mix_time = mix_back(
        (
            grad_recept_in,
            grad_decay_in,
            grad_key_in,
            value_input_gradient_first + grad_value_in_b,
            grad_rate_in,
            grad_gate_in,
        )
    )
    grad_rows_one, grad_edge_one = prev_one_back(grad_before_one)
    edge_back_one = shifted_2(grad_edge_one, "sa", -1)
    grad_normed_one = (
        grad_normed_one
        + grad_rows_one
        + jnp.concatenate(
            [jnp.zeros((length - 1, model_width), jnp.float32), edge_back_one], axis=0
        )
    )
    grad_input, grad_ln1_gain, grad_ln1_bias = ln_one_back(grad_normed_one)
    grad_input = grad_input + grad_mid
    grads = (
        grad_ln1_gain,
        grad_ln1_bias,
        grad_mix_time,
        grad_w_receptance,
        grad_w_key,
        grad_w_value,
        grad_w_output,
        grad_decay_base,
        grad_decay_down,
        decay_second_factor_gradient,
        grad_rate_base,
        grad_rate_down,
        rate_second_factor_gradient,
        value_residual_logits_gradient,
        value_residual_first_gradient,
        value_residual_second_gradient,
        grad_gate_down,
        grad_gate_up,
        grad_key_norm,
        grad_key_rate,
        present_token_boost_slope,
        grad_lnx_gain,
        grad_lnx_bias,
        grad_ln2_gain,
        grad_ln2_bias,
        grad_mix_channel,
        grad_ffn_key,
        grad_ffn_value,
    )
    owners = lax.axis_size("wa")
    small_places = [i for i in range(len(grads)) if i not in BIG]
    low = [grad.astype(jnp.bfloat16) for grad in grads]
    flat = jnp.concatenate([low[i].reshape(owners, -1) for i in small_places], axis=1)
    packed = jnp.concatenate(
        [low[i] for i in SQUARE] + [small_rows(flat, model_width // owners)], axis=1
    )
    packed, key_part = lax.optimization_barrier((packed, key_part))
    packed, key_part, value_part = lax.psum((scattered(packed), key_part, value_part), "sa")
    packed = packed.astype(jnp.float32)
    summed = {
        26: key_part.reshape(-1).astype(jnp.float32),
        27: value_part.reshape(-1).astype(jnp.float32),
    }
    at = 0
    for i in SQUARE:
        summed[i] = packed[:, at : at + model_width].reshape(-1)
        at += model_width
    packed = packed[:, at:].reshape(-1)
    at = 0
    for i in small_places:
        n = grads[i].size // owners
        summed[i] = packed[at : at + n]
        at += n
    summed = tuple((summed[i] for i in range(len(grads))))
    return (block_out.astype(jnp.bfloat16), grad_input, grad_first) + summed


def solution(mesh):
    return jax.shard_map(
        body,
        mesh=mesh,
        in_specs=(
            P(("wa", "sa"), None),
            P(("wa", "sa"), None),
            P(("wa", "sa")),
            P(("wa", "sa"), None),
            P("wa"),
            P("wa"),
            P("wa"),
            P("wa"),
            P("wa"),
            P("wa"),
            P("wa"),
            P("wa"),
            P("wa"),
            P("wa"),
            P("wa"),
            P("wa"),
            P("wa"),
            P("wa"),
            P("wa"),
            P("wa"),
            P("wa"),
            P("wa"),
            P("wa"),
            P("wa"),
            P("wa"),
            P("wa"),
            P("wa"),
            P("wa"),
            P("wa"),
            P("wa"),
            P("wa"),
            P("wa"),
        ),
        out_specs=(
            P(("wa", "sa"), None),
            P(("wa", "sa"), None),
            P(("wa", "sa"), None),
            P("wa"),
            P("wa"),
            P("wa"),
            P("wa"),
            P("wa"),
            P("wa"),
            P("wa"),
            P("wa"),
            P("wa"),
            P("wa"),
            P("wa"),
            P("wa"),
            P("wa"),
            P("wa"),
            P("wa"),
            P("wa"),
            P("wa"),
            P("wa"),
            P("wa"),
            P("wa"),
            P("wa"),
            P("wa"),
            P("wa"),
            P("wa"),
            P("wa"),
            P("wa"),
            P("wa"),
            P("wa"),
        ),
        check_vma=False,
    )
```
